256 devices in a mesh: tm: 8 (over y, core), space: 32 (over z, x).
Axes of the slice: x: 4, y: 4, z: 8, core: 2. Of those that a mesh axis runs over, the one named last changes fastest.
Arguments:
- node_states: float32 [8, 9, 131072], P('tm', None, 'space'), may hold values from -6 to 6
- strengths: float32 [3, 131072], P(None, 'space'), may hold values from -4 to 4
- start_state: float32 [3, 131072], P(None, 'space'), may hold values from -6 to 6
- lists: int32 [1024, 12], replicated, may hold values from 0 to 1023, as said below
- counts: int32 [32], replicated, may hold values from 16 to 32, as said below
Outputs:
- new_nodes: float32 [8, 9, 131072], P('tm', None, 'space')
The draws below stay inside these ranges and needn't reach their ends.
Inputs may be any that keep to these rules, and one draw needn't show every extreme that they name: `lists`: every entry names a live block; the entries of one row are distinct; over all rows of one shard, live or not, each other shard has between 1 and 2 distinct blocks named, and some pair of shards reaches 2; a shard's own blocks may be named freely. `counts`: number of live blocks of each shard; slots from that number to 31 hold no particles that matter.
All inputs are finite; a program needn't handle non-finite values.
Results may differ from the reference program's by a relative error of at most 0.00005.
Values sent between devices are 32-bit elements; how exact they have to be, the bound alone decides.
No kernel may reach another device: no remote copies, remote signals or barrier semaphores. Data moves between devices by JAX's collectives and lax.ppermute only.
A program may use at most 64 MiB of HBM per device.

```python
import math
import jax
import jax.numpy as jnp
import numpy as np
from jax import lax

BLK = 128
LIST = 12
CAP = 2
BLK_DEV = 32
NBLK = 1024
NP = 131072
N_TM = 8
N_SPACE = 32


def shared_lists(key):
    folded = jax.random.fold_in(key, 7)
    streams = jax.random.split(folded, 8)
    shard_ids = jnp.arange(N_SPACE, dtype=jnp.int32)
    counts = jax.random.randint(streams[0], (N_SPACE,), BLK_DEV // 2, BLK_DEV + 1)
    top_rank = jax.random.randint(streams[1], (), 0, N_SPACE)
    low_rank = (top_rank + 1 + jax.random.randint(streams[2], (), 0, N_SPACE - 1)) % N_SPACE
    counts = jnp.where(shard_ids == top_rank, BLK_DEV, counts)
    counts = jnp.where(shard_ids == low_rank, BLK_DEV // 2, counts)
    local_ids = jnp.arange(BLK_DEV, dtype=jnp.int32)
    empty_slot = (local_ids[None, None, :] >= counts[None, :, None]).astype(jnp.int32)
    jitter = jax.random.randint(streams[3], (N_SPACE, N_SPACE, BLK_DEV), 0, 4096)
    ordering = empty_slot * (1 << 24) + jitter * BLK_DEV + local_ids[None, None, :]
    chosen = jnp.argsort(ordering, axis=-1, stable=True)[:, :, :CAP]
    remote = shard_ids[None, :, None] * BLK_DEV + chosen
    per_pair = jax.random.randint(streams[4], (N_SPACE, N_SPACE), 1, CAP + 1)
    pair_recv = jax.random.randint(streams[5], (), 0, N_SPACE)
    pair_send = (pair_recv + 1 + jax.random.randint(streams[6], (), 0, N_SPACE - 1)) % N_SPACE
    per_pair = jnp.where((shard_ids[:, None] == pair_recv) & (shard_ids[None, :] == pair_send), CAP, per_pair)
    slot_ids = jnp.arange(CAP, dtype=jnp.int32)
    remote_ok = (slot_ids[None, None, :] < per_pair[:, :, None]) & (shard_ids[:, None, None] != shard_ids[None, :, None])
    own_ids = shard_ids[:, None] * BLK_DEV + local_ids[None, :]
    own_ok = local_ids[None, :] < counts[:, None]
    candidates = jnp.concatenate([own_ids, remote.reshape(N_SPACE, N_SPACE * CAP)], axis=1)
    usable = jnp.concatenate([own_ok, remote_ok.reshape(N_SPACE, N_SPACE * CAP)], axis=1).astype(jnp.int32)
    span_all = BLK_DEV + N_SPACE * CAP
    places = jnp.arange(span_all, dtype=jnp.int32)
    shuffle = jax.random.randint(streams[7], (N_SPACE, span_all), 0, 4096)
    shuffled = jnp.argsort((1 - usable) * (1 << 24) + shuffle * span_all + places[None, :], axis=-1, stable=True)
    ordered = jnp.take_along_axis(candidates, shuffled, axis=1)
    set_sizes = jnp.sum(usable, axis=1)
    positions = local_ids[:, None] * LIST + jnp.arange(LIST, dtype=jnp.int32)[None, :]
    positions = positions[None] % set_sizes[:, None, None]
    listing = jnp.take_along_axis(ordered, positions.reshape(N_SPACE, BLK_DEV * LIST), axis=1)
    return (listing.reshape(N_SPACE * BLK_DEV, LIST).astype(jnp.int32), counts.astype(jnp.int32))


def draw_lists(key, part):
    return shared_lists(key)[0]


def draw_counts(key, part):
    return shared_lists(key)[1]


def block_scale(rng, dims, cuts, low, largest):
    gain = 1.0
    for dim, parts in cuts:
        heights = jax.random.uniform(jax.random.fold_in(jax.random.fold_in(rng, 6), dim), (parts,), jnp.float32, low / len(cuts), largest / len(cuts))
        gain = gain * jnp.repeat(jnp.exp(heights), dims[dim] // parts).reshape((-1,) + (1,) * (len(dims) - 1 - dim))
    return gain


def scatter_about(rng, extent, spread, most, pieces=(), kind=jnp.bfloat16):
    drawn = spread * jax.random.normal(rng, extent, jnp.float32)
    if pieces:
        drawn = drawn * block_scale(rng, extent, pieces, -0.22, 0.18)
    return jnp.clip(drawn, -most, most).astype(kind)


def setup_inputs(seed: int = 0) -> dict:
    arg_keys = jax.random.split(jax.random.key(seed), 6)
    node_states = scatter_about(arg_keys[0], (N_TM, 9, NP), 1.0, 6.0, ((0, 8), (2, 32)), jnp.float32)
    strengths = scatter_about(arg_keys[1], (3, NP), 0.5, 4.0, ((1, 32),), jnp.float32)
    start_state = scatter_about(arg_keys[2], (3, NP), 1.0, 6.0, ((1, 32),), jnp.float32)
    lists = draw_lists(jax.random.fold_in(arg_keys[5], 71), 0)
    counts = draw_counts(jax.random.fold_in(arg_keys[5], 71), 0)
    return dict(node_states=node_states, strengths=strengths, start_state=start_state, lists=lists, counts=counts)


core_sq = 0.25
step_size = 1.0

def radau_matrix():
    sqrt_six = math.sqrt(6.0)
    return np.array([[(88.0 - 7.0 * sqrt_six) / 360.0, (296.0 - 169.0 * sqrt_six) / 1800.0, (-2.0 + 3.0 * sqrt_six) / 225.0], [(296.0 + 169.0 * sqrt_six) / 1800.0, (88.0 + 7.0 * sqrt_six) / 360.0, (-2.0 - 3.0 * sqrt_six) / 225.0], [(16.0 - sqrt_six) / 36.0, (16.0 + sqrt_six) / 36.0, 1.0 / 9.0]])

def cross_rows(former, latter):
    return jnp.stack([former[:, 1] * latter[:, 2] - former[:, 2] * latter[:, 1], former[:, 2] * latter[:, 0] - former[:, 0] * latter[:, 2], former[:, 0] * latter[:, 1] - former[:, 1] * latter[:, 0]], axis=1)

def block_velocity(targets, sources):
    listed = jnp.transpose(sources, (1, 0, 2)).reshape(12, -1)
    places = listed[:9].reshape(3, 3, -1)
    strength = listed[9:]
    target_pos = targets.reshape(3, 3, -1)
    offset = target_pos[:, :, None, :] - places[:, :, :, None]
    kernel = (lax.optimization_barrier(jnp.sum(offset * offset, axis=1)) + core_sq) ** (-1.5)
    terms = cross_rows(offset, strength[None, :, :, None])
    velocity = lax.optimization_barrier(jnp.sum(kernel[:, None] * terms, axis=2))
    return (velocity * (-0.25 / math.pi)).reshape(9, -1)

def reference(node_states, strengths, start_state, lists, counts):
    slices = node_states.shape[0]
    payload = jnp.concatenate([node_states, jnp.broadcast_to(strengths[None], (slices, 3, strengths.shape[1]))], axis=1)
    blocks = payload.reshape(slices, 12, NBLK, BLK).transpose(0, 2, 1, 3)
    block_ids = jnp.arange(NBLK, dtype=jnp.int32)
    live_mask = block_ids % BLK_DEV < counts[block_ids // BLK_DEV]
    grouped = block_ids.reshape(NBLK // BLK_DEV, BLK_DEV)

    def one_slice(slice_data):

        def one_group(members):
            return jax.vmap(lambda target: block_velocity(slice_data[target, :9], slice_data[lists[target]]))(members)
        return lax.map(one_group, grouped).reshape(NBLK, 9, BLK)
    velocity = lax.map(one_slice, blocks)
    velocity = jnp.where(live_mask[None, :, None, None], velocity, jnp.zeros_like(velocity))
    rates = velocity.transpose(0, 2, 1, 3).reshape(slices, 3, 3, NBLK * BLK)
    table = jnp.asarray(radau_matrix(), jnp.float32)
    quadrature = step_size * jnp.einsum('mj,njcp->nmcp', table, rates, precision=lax.Precision.HIGHEST)
    increment = quadrature[:, 2]
    carried = jnp.concatenate([jnp.zeros_like(increment[:1]), jnp.cumsum(increment, axis=0)[:-1]], axis=0)
    updated = start_state[None, None] + carried[:, None] + quadrature
    return updated.reshape(slices, 9, NBLK * BLK)
```

```python
import math

import jax
import jax.numpy as jnp
import numpy as np
from jax import lax
from jax.experimental import pallas as pl
from jax.experimental.pallas import tpu as pltpu
from jax.sharding import PartitionSpec as P

core_sq = 0.25
step_size = 1.0
LANES = 128
ROWS = 16
bf16 = jnp.bfloat16
f32 = jnp.float32


def radau_matrix():
    sqrt_six = math.sqrt(6.0)
    return np.array(
        [
            [
                (88.0 - 7.0 * sqrt_six) / 360.0,
                (296.0 - 169.0 * sqrt_six) / 1800.0,
                (-2.0 + 3.0 * sqrt_six) / 225.0,
            ],
            [
                (296.0 + 169.0 * sqrt_six) / 1800.0,
                (88.0 + 7.0 * sqrt_six) / 360.0,
                (-2.0 - 3.0 * sqrt_six) / 225.0,
            ],
            [(16.0 - sqrt_six) / 36.0, (16.0 + sqrt_six) / 36.0, 1.0 / 9.0],
        ]
    )


def pieces(value):
    first = value.astype(bf16)
    rest = value - first.astype(f32)
    second = rest.astype(bf16)
    third = (rest - second.astype(f32)).astype(bf16)
    return first, second, third


def norm_rows(rows, extra):
    square = rows * rows
    norm = square + pltpu.roll(square, ROWS - 1, 0) + pltpu.roll(square, ROWS - 2, 0) + extra
    first, second, third = [piece.astype(f32) for piece in pieces(norm)]
    place = lax.broadcasted_iota(jnp.int32, (ROWS, LANES), 0) % 3
    return jnp.where(
        place == 0,
        first,
        jnp.where(place == 1, pltpu.roll(second, 1, 0), pltpu.roll(third, 2, 0)),
    )


def cross(former, latter):
    return [
        former[1] * latter[2] - former[2] * latter[1],
        former[2] * latter[0] - former[0] * latter[2],
        former[0] * latter[1] - former[1] * latter[0],
    ]


def source_features(rows, feature_ref, weight_ref, slot):
    first, second, third = [(-2.0 * piece.astype(f32)).astype(bf16) for piece in pieces(rows)]
    norms = norm_rows(rows, core_sq).astype(bf16)
    ones = jnp.ones((ROWS, LANES), bf16)
    stacked = jnp.concatenate([first, second, first, second, third, first, norms, ones], 0)
    feature_ref[slot] = stacked.T
    strength = [rows[9 + c : 10 + c] for c in range(3)]
    blank = jnp.zeros((2, LANES), f32)
    for m in range(3):
        place = [rows[3 * m + c : 3 * m + c + 1] for c in range(3)]
        weights = jnp.concatenate(strength + cross(place, strength) + [blank], 0)
        parts = [piece.astype(f32) for piece in pieces(weights)]
        weight_ref[slot, m] = jnp.concatenate(parts + [jnp.zeros((8, LANES), f32)], 0).astype(bf16)


def target_features(rows):
    first, second, third = [piece.astype(f32) for piece in pieces(rows)]
    norms = norm_rows(rows, 0.0)
    place = lax.broadcasted_iota(jnp.int32, (ROWS, LANES), 0)
    ones = jnp.ones((ROWS, LANES), f32)
    groups = (first, first, second, second, first, third, ones, norms)
    made = []
    for m in range(3):
        node = (place >= 3 * m) & (place < 3 * m + 3)
        made.append(jnp.concatenate([jnp.where(node, g, 0.0).astype(bf16) for g in groups], 0))
    return made


def gather_kernel(pick_ref, own_ref, send_ref):
    def one(d, _):
        send_ref[d, 0:12] = own_ref[pick_ref[0, d], 0:12]
        send_ref[d, 12:24] = own_ref[pick_ref[1, d], 0:12]
        return 0

    lax.fori_loop(0, send_ref.shape[0], one, 0)


def rates_kernel(
    table_ref, live_ref, own_ref, far_ref, start_ref, base_ref, step_ref, feature_ref, weight_ref
):
    blocks = own_ref.shape[0]
    shards_count = far_ref.shape[0]
    list_len = table_ref.shape[0] // blocks
    radau = radau_matrix() * step_size

    def own_source(i, _):
        source_features(own_ref[i], feature_ref, weight_ref, i)
        return 0

    def far_source(i, _):
        blank = jnp.zeros((4, LANES), f32)
        for k in range(2):
            rows = jnp.concatenate([far_ref[i, 12 * k : 12 * k + 12], blank], 0)
            source_features(rows, feature_ref, weight_ref, blocks + 2 * i + k)
        return 0

    lax.fori_loop(0, blocks, own_source, 0)
    lax.fori_loop(0, shards_count, far_source, 0)
    live = live_ref[0]

    def pair(i, _):
        ids = (2 * i, 2 * i + 1)
        rows = [own_ref[t] for t in ids]
        targets = [target_features(r) for r in rows]
        slots = [[table_ref[t * list_len + j] for j in range(list_len)] for t in ids]
        zero = jnp.zeros((LANES, LANES), bf16)
        velocity = ([], [])
        for m in range(3):
            both = jnp.concatenate(
                [
                    jnp.concatenate([targets[0][m], zero], 1),
                    jnp.concatenate([zero, targets[1][m]], 1),
                ],
                0,
            )
            total = jnp.zeros((64, 2 * LANES), f32)
            for j in range(0, list_len, 2):
                features = jnp.concatenate(
                    [
                        jnp.concatenate([feature_ref[slots[0][q]], feature_ref[slots[1][q]]], 1)
                        for q in (j, j + 1)
                    ],
                    0,
                )
                weights = jnp.concatenate(
                    [
                        jnp.concatenate([weight_ref[s[j], m], weight_ref[s[j + 1], m]], 1)
                        for s in slots
                    ],
                    0,
                )
                squares = jnp.dot(features, both, preferred_element_type=f32)
                inverse = lax.rsqrt(squares)
                kernel = inverse * inverse * inverse
                high = kernel.astype(bf16)
                low = (kernel - high.astype(f32)).astype(bf16)
                total = total + jnp.dot(weights, high, preferred_element_type=f32)
                total = total + jnp.dot(weights, low, preferred_element_type=f32)
            for q in range(2):
                mine = total[32 * q : 32 * q + 32, LANES * q : LANES * q + LANES]
                sums = mine[0:8] + mine[8:16] + mine[16:24]
                place = [rows[q][3 * m + c : 3 * m + c + 1] for c in range(3)]
                spread = cross(place, [sums[c : c + 1] for c in range(3)])
                velocity[q].append(
                    [(spread[c] - sums[3 + c : 4 + c]) * (-0.25 / math.pi) for c in range(3)]
                )
        for q in range(2):
            t = ids[q]
            on = jnp.where(t < live, 1.0, 0.0).astype(f32)
            lanes = pl.ds(pl.multiple_of(t * LANES, LANES), LANES)
            start = start_ref[:, lanes]
            for k in range(3):
                step = [
                    sum(float(radau[k, n]) * velocity[q][n][c] for n in range(3)) * on
                    for c in range(3)
                ]
                step = jnp.concatenate(step, 0)
                base_ref[3 * k : 3 * k + 3, lanes] = start + step
                if k == 2:
                    step_ref[:, lanes] = step
        return 0

    lax.fori_loop(0, blocks // 2, pair, 0)


def vmem():
    return pl.BlockSpec(memory_space=pltpu.VMEM)


def smem():
    return pl.BlockSpec(memory_space=pltpu.SMEM)


def shards(node_states, strengths, start_state, lists, counts):
    groups = lax.axis_size("space")
    slices = lax.axis_size("tm")
    rank = lax.axis_index("space")
    blocks = lists.shape[0] // groups
    list_len = lists.shape[1]
    particles = node_states.shape[2]
    own = jnp.concatenate([node_states[0], strengths, jnp.zeros((4, particles), f32)], axis=0)
    own = own.reshape(ROWS, blocks, LANES).transpose(1, 0, 2)

    owner, block = lists // blocks, lists % blocks
    mine = owner == rank
    lowest = jnp.min(jnp.where(mine, block, blocks - 1).reshape(groups, -1), axis=1)
    highest = jnp.max(jnp.where(mine, block, 0).reshape(groups, -1), axis=1)
    send = pl.pallas_call(
        gather_kernel,
        out_shape=jax.ShapeDtypeStruct((groups, 24, LANES), f32),
        in_specs=[smem(), vmem()],
        out_specs=vmem(),
        name="gather_blocks",
    )(jnp.stack([lowest, highest]), own)
    far = lax.all_to_all(send, "space", 0, 0, tiled=True)

    my_lists = lax.dynamic_slice_in_dim(lists, rank * blocks, blocks, 0)
    owner, block = my_lists.reshape(-1) // blocks, my_lists.reshape(-1) % blocks
    from_shard = owner[None, :] == jnp.arange(groups, dtype=jnp.int32)[:, None]
    first = jnp.min(jnp.where(from_shard, block[None, :], blocks - 1), axis=1)
    first = jnp.sum(jnp.where(from_shard, first[:, None], 0), axis=0)
    table = jnp.where(
        owner == rank, block, blocks + 2 * owner + (block != first).astype(jnp.int32)
    )
    live = lax.dynamic_slice_in_dim(counts, rank, 1, 0)

    base, step = pl.pallas_call(
        rates_kernel,
        out_shape=(
            jax.ShapeDtypeStruct((9, particles), f32),
            jax.ShapeDtypeStruct((3, particles), f32),
        ),
        in_specs=[smem(), smem(), vmem(), vmem(), vmem()],
        out_specs=(vmem(), vmem()),
        scratch_shapes=[
            pltpu.VMEM((blocks + 2 * groups, LANES, LANES), bf16),
            pltpu.VMEM((blocks + 2 * groups, 3, 32, LANES), bf16),
        ],
        compiler_params=pltpu.CompilerParams(vmem_limit_bytes=56 << 20),
        name="rates",
    )(table, live, own, far, start_state)

    def earlier(value, shift):
        return lax.ppermute(value, "tm", [(i, i + shift) for i in range(slices - shift)])

    carried = earlier(step, 1)
    span, shift = step + carried, 2
    while shift < slices:
        got = earlier(span, shift)
        carried, span, shift = carried + got, span + got, 2 * shift
    new = base.reshape(3, 3, particles) + carried[None]
    return new.reshape(1, 9, particles)


def solution(mesh):
    return jax.shard_map(
        shards,
        mesh=mesh,
        in_specs=(P("tm", None, "space"), P(None, "space"), P(None, "space"), P(), P()),
        out_specs=P("tm", None, "space"),
        check_vma=False,
    )
```

```python
import functools
import math

import jax
import jax.numpy as jnp
import numpy as np
from jax import lax
from jax.experimental import pallas as pl
from jax.experimental.pallas import tpu as pltpu
from jax.sharding import PartitionSpec as P

core_sq = 0.25
step_size = 1.0
LANES = 128
ROWS = 16
MOST_EARLY = 3
bf16 = jnp.bfloat16
f32 = jnp.float32


def radau_matrix():
    sqrt_six = math.sqrt(6.0)
    return np.array(
        [
            [
                (88.0 - 7.0 * sqrt_six) / 360.0,
                (296.0 - 169.0 * sqrt_six) / 1800.0,
                (-2.0 + 3.0 * sqrt_six) / 225.0,
            ],
            [
                (296.0 + 169.0 * sqrt_six) / 1800.0,
                (88.0 + 7.0 * sqrt_six) / 360.0,
                (-2.0 - 3.0 * sqrt_six) / 225.0,
            ],
            [(16.0 - sqrt_six) / 36.0, (16.0 + sqrt_six) / 36.0, 1.0 / 9.0],
        ]
    )


def pieces(value):
    first = value.astype(bf16)
    rest = value - first.astype(f32)
    second = rest.astype(bf16)
    third = (rest - second.astype(f32)).astype(bf16)
    return first, second, third


def norm_rows(rows, extra):
    square = rows * rows
    norm = square + pltpu.roll(square, ROWS - 1, 0) + pltpu.roll(square, ROWS - 2, 0) + extra
    first, second, third = [piece.astype(f32) for piece in pieces(norm)]
    place = lax.broadcasted_iota(jnp.int32, (ROWS, LANES), 0) % 3
    return jnp.where(
        place == 0,
        first,
        jnp.where(place == 1, pltpu.roll(second, 1, 0), pltpu.roll(third, 2, 0)),
    )


def cross(former, latter):
    return [
        former[1] * latter[2] - former[2] * latter[1],
        former[2] * latter[0] - former[0] * latter[2],
        former[0] * latter[1] - former[1] * latter[0],
    ]


def source_features(rows, feature_ref, weight_ref, slot):
    first, second, third = [(-2.0 * piece.astype(f32)).astype(bf16) for piece in pieces(rows)]
    norms = norm_rows(rows, core_sq).astype(bf16)
    ones = jnp.ones((ROWS, LANES), bf16)
    stacked = jnp.concatenate([first, second, first, second, third, first, norms, ones], 0)
    feature_ref[slot] = stacked.T
    strength = [rows[9 + c : 10 + c] for c in range(3)]
    blank = jnp.zeros((2, LANES), f32)
    for m in range(3):
        place = [rows[3 * m + c : 3 * m + c + 1] for c in range(3)]
        weights = jnp.concatenate(strength + cross(place, strength) + [blank], 0)
        parts = [piece.astype(f32) for piece in pieces(weights)]
        weight_ref[slot, m] = jnp.concatenate(parts + [jnp.zeros((8, LANES), f32)], 0).astype(bf16)


def target_features(rows, target_ref, t):
    first, second, third = [piece.astype(f32) for piece in pieces(rows)]
    norms = norm_rows(rows, 0.0)
    place = lax.broadcasted_iota(jnp.int32, (ROWS, LANES), 0)
    ones = jnp.ones((ROWS, LANES), f32)
    groups = (first, first, second, second, first, third, ones, norms)
    for m in range(3):
        node = (place >= 3 * m) & (place < 3 * m + 3)
        target_ref[t, m] = jnp.concatenate(
            [jnp.where(node, g, 0.0).astype(bf16) for g in groups], 0
        )


def lanes_of(t):
    return pl.ds(pl.multiple_of(t * LANES, LANES), LANES)


def pair_sums(table_ref, target_ref, feature_ref, weight_ref, i, m, begin, end):
    list_len = table_ref.shape[0] // target_ref.shape[0]
    ids = (2 * i, 2 * i + 1)
    zero = jnp.zeros((LANES, LANES), bf16)
    both = jnp.concatenate(
        [
            jnp.concatenate([target_ref[ids[0], m], zero], 1),
            jnp.concatenate([zero, target_ref[ids[1], m]], 1),
        ],
        0,
    )
    total = jnp.zeros((64, 2 * LANES), f32)
    for j in range(begin, end, 2):
        slots = [[table_ref[t * list_len + q] for q in (j, j + 1)] for t in ids]
        features = jnp.concatenate(
            [
                jnp.concatenate([feature_ref[slots[0][q]], feature_ref[slots[1][q]]], 1)
                for q in range(2)
            ],
            0,
        )
        weights = jnp.concatenate(
            [jnp.concatenate([weight_ref[s[0], m], weight_ref[s[1], m]], 1) for s in slots], 0
        )
        squares = jnp.dot(features, both, preferred_element_type=f32)
        inverse = lax.rsqrt(squares)
        kernel = inverse * inverse * inverse
        high = kernel.astype(bf16)
        low = (kernel - high.astype(f32)).astype(bf16)
        total = total + jnp.dot(weights, high, preferred_element_type=f32)
        total = total + jnp.dot(weights, low, preferred_element_type=f32)
    sums = []
    for q in range(2):
        mine = total[32 * q : 32 * q + 32, LANES * q : LANES * q + LANES]
        sums.append(mine[0:8] + mine[8:16] + mine[16:24])
    return sums


def fetch(pairs, sems):
    copies = [pltpu.make_async_copy(a, b, sems.at[k]) for k, (a, b) in enumerate(pairs)]
    for copy in copies:
        copy.start()
    return copies


def gather_kernel(pick_ref, node_in, strength_in, send_ref, node_ref, strength_ref, sems):
    for copy in fetch(((node_in, node_ref), (strength_in, strength_ref)), sems):
        copy.wait()

    def one(d, _):
        for k in range(2):
            lanes = lanes_of(pick_ref[k, d])
            send_ref[d, 12 * k : 12 * k + 9] = node_ref[:, pick_ref[k, d], :]
            send_ref[d, 12 * k + 9 : 12 * k + 12] = strength_ref[:, lanes]
        return 0

    lax.fori_loop(0, send_ref.shape[0], one, 0, unroll=4)


def near_kernel(
    table_ref,
    early_ref,
    node_in,
    strength_in,
    feature_out,
    weight_out,
    target_out,
    part_out,
    feature_ref,
    weight_ref,
    target_ref,
    part_ref,
    node_ref,
    strength_ref,
    sems,
):
    blocks = part_ref.shape[0]
    for copy in fetch(((node_in, node_ref), (strength_in, strength_ref)), sems):
        copy.wait()

    def prepare(t, _):
        lanes = lanes_of(t)
        rows = jnp.concatenate(
            [node_ref[:, t, :], strength_ref[:, lanes], jnp.zeros((4, LANES), f32)], 0
        )
        source_features(rows, feature_ref, weight_ref, t)
        target_features(rows, target_ref, t)
        return 0

    lax.fori_loop(0, blocks, prepare, 0, unroll=4)
    kept = ((feature_ref, feature_out), (weight_ref, weight_out), (target_ref, target_out))
    copies = fetch(kept, sems)

    def pair(i, _):
        for steps in range(MOST_EARLY + 1):

            @pl.when(early_ref[i] == steps)
            def _():
                for m in range(3):
                    sums = pair_sums(
                        table_ref, target_ref, feature_ref, weight_ref, i, m, 0, 2 * steps
                    )
                    for q in range(2):
                        part_ref[2 * i + q, m] = sums[q]

        return 0

    lax.fori_loop(0, blocks // 2, pair, 0)
    copies.append(pltpu.make_async_copy(part_ref, part_out, sems.at[3]))
    copies[3].start()
    for copy in copies:
        copy.wait()


def rest_kernel(
    table_ref,
    early_ref,
    live_ref,
    far_ref,
    near_feature,
    near_weight,
    near_target,
    near_part,
    node_in,
    start_in,
    base_out,
    step_ref,
    feature_ref,
    weight_ref,
    target_ref,
    part_ref,
    node_ref,
    start_ref,
    base_ref,
    sems,
):
    blocks = part_ref.shape[0]
    list_len = table_ref.shape[0] // blocks
    radau = radau_matrix() * step_size

    def far_source(i, _):
        blank = jnp.zeros((4, LANES), f32)
        for k in range(2):
            rows = jnp.concatenate([far_ref[i, 12 * k : 12 * k + 12], blank], 0)
            source_features(rows, feature_ref, weight_ref, blocks + 2 * i + k)
        return 0

    kept = (
        (near_feature, feature_ref.at[0:blocks]),
        (near_weight, weight_ref.at[0:blocks]),
        (near_target, target_ref),
        (near_part, part_ref),
        (node_in, node_ref),
        (start_in, start_ref),
    )
    copies = fetch(kept, sems)
    lax.fori_loop(0, far_ref.shape[0], far_source, 0, unroll=2)
    for copy in copies:
        copy.wait()
    live = live_ref[0]

    def pair(i, _):
        for steps in range(MOST_EARLY + 1):

            @pl.when(early_ref[i] == steps)
            def _():
                finish(i, 2 * steps)

        return 0

    def finish(i, begin):
        lanes = [lanes_of(2 * i + q) for q in range(2)]
        rows = [node_ref[:, 2 * i + q, :] for q in range(2)]
        velocity = ([], [])
        for m in range(3):
            both = pair_sums(
                table_ref, target_ref, feature_ref, weight_ref, i, m, begin, list_len
            )
            for q in range(2):
                sums = both[q] + part_ref[2 * i + q, m]
                place = [rows[q][3 * m + c : 3 * m + c + 1] for c in range(3)]
                spread = cross(place, [sums[c : c + 1] for c in range(3)])
                velocity[q].append(
                    [(spread[c] - sums[3 + c : 4 + c]) * (-0.25 / math.pi) for c in range(3)]
                )
        for q in range(2):
            on = jnp.where(2 * i + q < live, 1.0, 0.0).astype(f32)
            start = start_ref[:, lanes[q]]
            for k in range(3):
                step = [
                    sum(float(radau[k, n]) * velocity[q][n][c] for n in range(3)) * on
                    for c in range(3)
                ]
                for c in range(3):
                    base_ref[3 * k + c, pl.ds(2 * i + q, 1), :] = start[c : c + 1] + step[c]
                    if k == 2:
                        step_ref[c, pl.ds(2 * i + q, 1), :] = step[c]

    half = blocks // 2
    copies = []
    for k in range(2):
        lax.fori_loop(k * half // 2, (k + 1) * half // 2, pair, 0)
        rows = pl.ds(k * half, half)
        copy = pltpu.make_async_copy(base_ref.at[:, rows], base_out.at[:, rows], sems.at[k])
        copy.start()
        copies.append(copy)
    for copy in copies:
        copy.wait()


def hbm():
    return pl.BlockSpec(memory_space=pltpu.HBM)


def in_hbm(value):
    return pltpu.with_memory_space_constraint(value, pltpu.HBM)


def vmem():
    return pl.BlockSpec(memory_space=pltpu.VMEM)


def smem():
    return pl.BlockSpec(memory_space=pltpu.SMEM)


def sum_kernel(shifts, base_in, other_ref, *refs):
    got_refs, (out_ref, base_ref, sems) = refs[:-3], refs[-3:]
    (copy,) = fetch(((base_in, base_ref),), sems)
    rank = lax.axis_index("tm")

    def keep(value, k):
        return jnp.where((rank ^ k) < rank, 1.0, 0.0).astype(f32) * value

    carried = keep(other_ref[...], 1)
    for k, ref in zip(shifts, got_refs):
        carried = carried + keep(ref[...], k)
    copy.wait()
    for m in range(3):
        out_ref[3 * m : 3 * m + 3] = base_ref[3 * m : 3 * m + 3] + carried


def add_earlier(base, step, slices):
    def swap(value, k):
        return lax.ppermute(value, "tm", [(i, i ^ k) for i in range(slices)])

    other = swap(step, 1)
    chip = step + other
    shifts = tuple(range(2, slices, 2))
    got = [swap(chip, k) for k in shifts]
    return pl.pallas_call(
        functools.partial(sum_kernel, shifts),
        out_shape=jax.ShapeDtypeStruct(base.shape, f32),
        in_specs=[hbm()] + [vmem()] * (1 + len(got)),
        out_specs=vmem(),
        scratch_shapes=[pltpu.VMEM(base.shape, f32), pltpu.SemaphoreType.DMA((1,))],
        compiler_params=pltpu.CompilerParams(vmem_limit_bytes=8 << 20),
        name="add_earlier",
    )(in_hbm(base), other, *got)


def shards(node_states, strengths, start_state, lists, counts):
    groups = lax.axis_size("space")
    slices = lax.axis_size("tm")
    rank = lax.axis_index("space")
    blocks = lists.shape[0] // groups
    list_len = lists.shape[1]
    nodes = in_hbm(node_states.reshape(9, blocks, LANES))
    strengths, start_state = in_hbm(strengths), in_hbm(start_state)

    owner, block = lists // blocks, lists % blocks
    mine = owner == rank
    lowest = jnp.min(jnp.where(mine, block, blocks - 1).reshape(groups, -1), axis=1)
    highest = jnp.max(jnp.where(mine, block, 0).reshape(groups, -1), axis=1)
    send = pl.pallas_call(
        gather_kernel,
        out_shape=jax.ShapeDtypeStruct((groups, 24, LANES), f32),
        in_specs=[smem(), hbm(), hbm()],
        out_specs=vmem(),
        scratch_shapes=[
            pltpu.VMEM((9, blocks, LANES), f32),
            pltpu.VMEM((3, blocks * LANES), f32),
            pltpu.SemaphoreType.DMA((2,)),
        ],
        compiler_params=pltpu.CompilerParams(vmem_limit_bytes=8 << 20),
        name="gather_blocks",
    )(jnp.stack([lowest, highest]), nodes, strengths)
    far = lax.all_to_all(send, "space", 0, 0, tiled=True)

    my_lists = lax.dynamic_slice_in_dim(lists, rank * blocks, blocks, 0)
    owner, block = my_lists.reshape(-1) // blocks, my_lists.reshape(-1) % blocks
    from_shard = owner[None, :] == jnp.arange(groups, dtype=jnp.int32)[:, None]
    first = jnp.min(jnp.where(from_shard, block[None, :], blocks - 1), axis=1)
    first = jnp.sum(jnp.where(from_shard, first[:, None], 0), axis=0)
    slot = jnp.where(
        owner == rank, block, blocks + 2 * owner + (block != first).astype(jnp.int32)
    ).reshape(blocks, list_len)
    near = (slot < blocks).astype(jnp.int32)
    order = jnp.arange(list_len, dtype=jnp.int32)
    ahead = order[None, :] < order[:, None]
    near_ahead = jnp.sum(jnp.where(ahead[None], near[:, None, :], 0), axis=2)
    near_count = jnp.sum(near, axis=1, keepdims=True)
    place = jnp.where(near == 1, near_ahead, near_count + order[None, :] - near_ahead)
    hit = place[:, None, :] == order[None, :, None]
    table = jnp.sum(jnp.where(hit, slot[:, None, :], 0), axis=2).reshape(-1)
    early = jnp.min(near_count.reshape(blocks // 2, 2), axis=1) // 2
    early = jnp.minimum(early, MOST_EARLY)
    live = lax.dynamic_slice_in_dim(counts, rank, 1, 0)

    kept = (
        ((blocks, LANES, LANES), bf16),
        ((blocks, 3, 32, LANES), bf16),
        ((blocks, 3, LANES, LANES), bf16),
        ((blocks, 3, 8, LANES), f32),
    )
    near_results = pl.pallas_call(
        near_kernel,
        out_shape=tuple(pltpu.HBM(*k) for k in kept),
        in_specs=[smem(), smem(), hbm(), hbm()],
        out_specs=(hbm(),) * 4,
        scratch_shapes=[pltpu.VMEM(*k) for k in kept]
        + [
            pltpu.VMEM((9, blocks, LANES), f32),
            pltpu.VMEM((3, blocks * LANES), f32),
            pltpu.SemaphoreType.DMA((4,)),
        ],
        compiler_params=pltpu.CompilerParams(vmem_limit_bytes=16 << 20),
        cost_estimate=pl.CostEstimate(
            flops=10_000_000_000, bytes_accessed=6_000_000, transcendentals=0
        ),
        name="near_rates",
    )(table, early, nodes, strengths)

    slots = blocks + 2 * groups
    base, step = pl.pallas_call(
        rest_kernel,
        out_shape=(
            pltpu.HBM((9, blocks, LANES), f32),
            jax.ShapeDtypeStruct((3, blocks, LANES), f32),
        ),
        in_specs=[smem()] * 3 + [vmem()] + [hbm()] * 6,
        out_specs=(hbm(), vmem()),
        scratch_shapes=[
            pltpu.VMEM((slots, LANES, LANES), bf16),
            pltpu.VMEM((slots, 3, 32, LANES), bf16),
            pltpu.VMEM(*kept[2]),
            pltpu.VMEM(*kept[3]),
            pltpu.VMEM((9, blocks, LANES), f32),
            pltpu.VMEM((3, blocks * LANES), f32),
            pltpu.VMEM((9, blocks, LANES), f32),
            pltpu.SemaphoreType.DMA((6,)),
        ],
        compiler_params=pltpu.CompilerParams(vmem_limit_bytes=24 << 20),
        name="rest_rates",
    )(table, early, live, far, *map(in_hbm, near_results), nodes, start_state)

    return add_earlier(base, step, slices).reshape(1, 9, blocks * LANES)


def solution(mesh):
    return jax.shard_map(
        shards,
        mesh=mesh,
        in_specs=(P("tm", None, "space"), P(None, "space"), P(None, "space"), P(), P()),
        out_specs=P("tm", None, "space"),
        check_vma=False,
    )
```

```python
import functools
import math

import jax
import jax.numpy as jnp
import numpy as np
from jax import lax
from jax.experimental import pallas as pl
from jax.experimental.pallas import tpu as pltpu
from jax.sharding import PartitionSpec as P

core_sq = 0.25
step_size = 1.0
LANES = 128
ROWS = 16
LIST = 12
TOGETHER = 4
MOST_EARLY = 2
bf16 = jnp.bfloat16
f32 = jnp.float32


def radau_matrix():
    sqrt_six = math.sqrt(6.0)
    return np.array(
        [
            [
                (88.0 - 7.0 * sqrt_six) / 360.0,
                (296.0 - 169.0 * sqrt_six) / 1800.0,
                (-2.0 + 3.0 * sqrt_six) / 225.0,
            ],
            [
                (296.0 + 169.0 * sqrt_six) / 1800.0,
                (88.0 + 7.0 * sqrt_six) / 360.0,
                (-2.0 - 3.0 * sqrt_six) / 225.0,
            ],
            [(16.0 - sqrt_six) / 36.0, (16.0 + sqrt_six) / 36.0, 1.0 / 9.0],
        ]
    )


def pieces(value):
    first = value.astype(bf16)
    rest = value - first.astype(f32)
    second = rest.astype(bf16)
    third = (rest - second.astype(f32)).astype(bf16)
    return first, second, third


def norm_rows(rows, extra):
    square = rows * rows
    norm = square + pltpu.roll(square, ROWS - 1, 0) + pltpu.roll(square, ROWS - 2, 0) + extra
    first, second, third = [piece.astype(f32) for piece in pieces(norm)]
    place = lax.broadcasted_iota(jnp.int32, (ROWS, LANES), 0) % 3
    return jnp.where(
        place == 0,
        first,
        jnp.where(place == 1, pltpu.roll(second, 1, 0), pltpu.roll(third, 2, 0)),
    )


def cross(former, latter):
    return [
        former[1] * latter[2] - former[2] * latter[1],
        former[2] * latter[0] - former[0] * latter[2],
        former[0] * latter[1] - former[1] * latter[0],
    ]


def source_features(rows, feature_ref, weight_ref, slot):
    first, second, third = [(-2.0 * piece.astype(f32)).astype(bf16) for piece in pieces(rows)]
    norms = norm_rows(rows, core_sq).astype(bf16)
    ones = jnp.ones((ROWS, LANES), bf16)
    stacked = jnp.concatenate([first, second, first, second, third, first, norms, ones], 0)
    feature_ref[slot] = stacked.T
    place = lax.broadcasted_iota(jnp.int32, (ROWS, LANES), 0)

    def turned(value):
        ahead = jnp.where(place % 3 == 2, pltpu.roll(value, 2, 0), pltpu.roll(value, ROWS - 1, 0))
        behind = jnp.where(place % 3 == 0, pltpu.roll(value, ROWS - 2, 0), pltpu.roll(value, 1, 0))
        return ahead, behind

    strength = jnp.where(
        place < 3,
        pltpu.roll(rows, ROWS - 9, 0),
        jnp.where(place < 6, pltpu.roll(rows, ROWS - 6, 0), pltpu.roll(rows, ROWS - 3, 0)),
    )
    ahead, behind = turned(rows)
    strength_ahead, strength_behind = turned(strength)
    weights = jnp.where(place < 9, ahead * strength_behind - behind * strength_ahead, rows)
    parts = [piece.astype(f32) for piece in pieces(weights)]
    top = place < 3
    blank = jnp.zeros((8, LANES), f32)
    for m in range(3):
        made = [
            jnp.where(top, pltpu.roll(p, (ROWS - 3 * m) % ROWS, 0), pltpu.roll(p, ROWS - 6, 0))[0:8]
            for p in parts
        ]
        weight_ref[slot, m] = jnp.concatenate(made + [blank], 0).astype(bf16)


def target_features(rows, target_ref, t):
    first, second, third = [piece.astype(f32) for piece in pieces(rows)]
    norms = norm_rows(rows, 0.0)
    place = lax.broadcasted_iota(jnp.int32, (ROWS, LANES), 0)
    ones = jnp.ones((ROWS, LANES), f32)
    groups = (first, first, second, second, first, third, ones, norms)
    for m in range(3):
        node = (place >= 3 * m) & (place < 3 * m + 3)
        target_ref[t, m] = jnp.concatenate(
            [jnp.where(node, g, 0.0).astype(bf16) for g in groups], 0
        )


def lanes_of(t):
    return pl.ds(pl.multiple_of(t * LANES, LANES), LANES)


def pair_sums(table_ref, target_ref, feature_ref, weight_ref, ids, m, begin, end):
    list_len = LIST
    zero = jnp.zeros((LANES, LANES), bf16)
    both = jnp.concatenate(
        [
            jnp.concatenate([target_ref[ids[0], m], zero], 1),
            jnp.concatenate([zero, target_ref[ids[1], m]], 1),
        ],
        0,
    )
    total = jnp.zeros((64, 2 * LANES), f32)
    for j in range(begin, end, 2):
        slots = [[table_ref[t * list_len + q] for q in (j, j + 1)] for t in ids]
        features = jnp.concatenate(
            [
                jnp.concatenate([feature_ref[slots[0][q]], feature_ref[slots[1][q]]], 1)
                for q in range(2)
            ],
            0,
        )
        weights = jnp.concatenate(
            [jnp.concatenate([weight_ref[s[0], m], weight_ref[s[1], m]], 1) for s in slots], 0
        )
        squares = jnp.dot(features, both, preferred_element_type=f32)
        inverse = lax.rsqrt(squares)
        kernel = inverse * inverse * inverse
        high = kernel.astype(bf16)
        low = (kernel - high.astype(f32)).astype(bf16)
        total = total + jnp.dot(weights, high, preferred_element_type=f32)
        total = total + jnp.dot(weights, low, preferred_element_type=f32)
    sums = []
    for q in range(2):
        mine = total[32 * q : 32 * q + 32, LANES * q : LANES * q + LANES]
        sums.append(mine[0:8] + mine[8:16] + mine[16:24])
    return sums


def fetch(pairs, sems):
    copies = [pltpu.make_async_copy(a, b, sems.at[k]) for k, (a, b) in enumerate(pairs)]
    for copy in copies:
        copy.start()
    return copies


def group_pairs(table_ref, early, blocks, i):
    first = early + blocks // (2 * TOGETHER) + 2 * TOGETHER * i
    ids = [table_ref[first + k] for k in range(2 * TOGETHER)]
    return [(ids[2 * k], ids[2 * k + 1]) for k in range(TOGETHER)]


def gather_kernel(pick_ref, node_in, strength_in, send_ref, node_ref, strength_ref, sems):
    for copy in fetch(((node_in, node_ref), (strength_in, strength_ref)), sems):
        copy.wait()

    def one(d, _):
        for k in range(2):
            lanes = lanes_of(pick_ref[k, d])
            send_ref[d, 12 * k : 12 * k + 9] = node_ref[:, pick_ref[k, d], :]
            send_ref[d, 12 * k + 9 : 12 * k + 12] = strength_ref[:, lanes]
        return 0

    lax.fori_loop(0, send_ref.shape[0], one, 0, unroll=4)


def near_kernel(
    table_ref,
    node_in,
    strength_in,
    feature_out,
    weight_out,
    target_out,
    part_out,
    feature_ref,
    weight_ref,
    target_ref,
    part_ref,
    node_ref,
    strength_ref,
    sems,
):
    blocks = part_ref.shape[0]
    early = LIST * blocks
    for copy in fetch(((node_in, node_ref), (strength_in, strength_ref)), sems):
        copy.wait()

    def prepare(t, _):
        lanes = lanes_of(t)
        rows = jnp.concatenate(
            [node_ref[:, t, :], strength_ref[:, lanes], jnp.zeros((4, LANES), f32)], 0
        )
        source_features(rows, feature_ref, weight_ref, t)
        target_features(rows, target_ref, t)
        return 0

    lax.fori_loop(0, blocks, prepare, 0, unroll=4)
    kept = ((feature_ref, feature_out), (weight_ref, weight_out), (target_ref, target_out))
    copies = fetch(kept, sems)

    def group(i, _):
        for steps in range(MOST_EARLY + 1):

            @pl.when(table_ref[early + i] == steps)
            def _():
                made = []
                for ids in group_pairs(table_ref, early, blocks, i):
                    for m in range(3):
                        sums = pair_sums(
                            table_ref, target_ref, feature_ref, weight_ref, ids, m, 0, 2 * steps
                        )
                        made.extend((t, m, value) for t, value in zip(ids, sums))
                for t, m, value in made:
                    part_ref[t, m] = value

        return 0

    lax.fori_loop(0, blocks // (2 * TOGETHER), group, 0)
    copies.append(pltpu.make_async_copy(part_ref, part_out, sems.at[3]))
    copies[3].start()
    for copy in copies:
        copy.wait()


def rest_kernel(
    table_ref,
    count_ref,
    far_ref,
    near_feature,
    near_weight,
    near_target,
    near_part,
    node_in,
    start_in,
    base_out,
    step_ref,
    feature_ref,
    weight_ref,
    target_ref,
    part_ref,
    node_ref,
    start_ref,
    base_ref,
    sems,
):
    blocks = part_ref.shape[0]
    early = LIST * blocks
    radau = radau_matrix() * step_size

    def far_source(i, _):
        blank = jnp.zeros((4, LANES), f32)
        for k in range(2):
            rows = jnp.concatenate([far_ref[i, 12 * k : 12 * k + 12], blank], 0)
            source_features(rows, feature_ref, weight_ref, blocks + 2 * i + k)
        return 0

    kept = (
        (near_feature, feature_ref.at[0:blocks]),
        (near_weight, weight_ref.at[0:blocks]),
        (near_target, target_ref),
        (near_part, part_ref),
        (node_in, node_ref),
        (start_in, start_ref),
    )
    copies = fetch(kept, sems)
    lax.fori_loop(0, far_ref.shape[0], far_source, 0, unroll=2)
    for copy in copies:
        copy.wait()
    live = count_ref[lax.axis_index("space")]

    def group(i, _):
        for steps in range(MOST_EARLY + 1):

            @pl.when(table_ref[early + i] == steps)
            def _():
                made = []
                for ids in group_pairs(table_ref, early, blocks, i):
                    for m in range(3):
                        sums = pair_sums(
                            table_ref, target_ref, feature_ref, weight_ref, ids, m, 2 * steps, LIST
                        )
                        made.extend((t, m, value) for t, value in zip(ids, sums))
                for t, m, value in made:
                    part_ref[t, m] = part_ref[t, m] + value

        return 0

    def close(t, _):
        rows = node_ref[:, t, :]
        start = start_ref[:, lanes_of(t)]
        on = jnp.where(t < live, 1.0, 0.0).astype(f32)
        velocity = []
        for m in range(3):
            sums = part_ref[t, m]
            place = [rows[3 * m + c : 3 * m + c + 1] for c in range(3)]
            spread = cross(place, [sums[3 + c : 4 + c] for c in range(3)])
            velocity.append([(spread[c] - sums[c : c + 1]) * (-0.25 / math.pi) for c in range(3)])
        for k in range(3):
            for c in range(3):
                step = sum(float(radau[k, n]) * velocity[n][c] for n in range(3)) * on
                base_ref[3 * k + c, pl.ds(t, 1), :] = start[c : c + 1] + step
                if k == 2:
                    step_ref[c, pl.ds(t, 1), :] = step
        return 0

    lax.fori_loop(0, blocks // (2 * TOGETHER), group, 0)
    lax.fori_loop(0, blocks, close, 0, unroll=4)
    (copy,) = fetch(((base_ref, base_out),), sems)
    copy.wait()


def hbm():
    return pl.BlockSpec(memory_space=pltpu.HBM)


def in_hbm(value):
    return pltpu.with_memory_space_constraint(value, pltpu.HBM)


def vmem():
    return pl.BlockSpec(memory_space=pltpu.VMEM)


def smem():
    return pl.BlockSpec(memory_space=pltpu.SMEM)


def sum_kernel(shifts, base_in, other_ref, *refs):
    got_refs, (out_ref, base_ref, sems) = refs[:-3], refs[-3:]
    (copy,) = fetch(((base_in, base_ref),), sems)
    rank = lax.axis_index("tm")

    def keep(value, k):
        return jnp.where((rank ^ k) < rank, 1.0, 0.0).astype(f32) * value

    carried = keep(other_ref[...], 1)
    for k, ref in zip(shifts, got_refs):
        carried = carried + keep(ref[...], k)
    copy.wait()
    for m in range(3):
        out_ref[3 * m : 3 * m + 3] = base_ref[3 * m : 3 * m + 3] + carried


def add_earlier(base, step, slices):
    def swap(value, k):
        return lax.ppermute(value, "tm", [(i, i ^ k) for i in range(slices)])

    other = swap(step, 1)
    chip = step + other
    shifts = tuple(range(2, slices, 2))
    got = [swap(chip, k) for k in shifts]
    return pl.pallas_call(
        functools.partial(sum_kernel, shifts),
        out_shape=jax.ShapeDtypeStruct(base.shape, f32),
        in_specs=[hbm()] + [vmem()] * (1 + len(got)),
        out_specs=vmem(),
        scratch_shapes=[pltpu.VMEM(base.shape, f32), pltpu.SemaphoreType.DMA((1,))],
        compiler_params=pltpu.CompilerParams(vmem_limit_bytes=8 << 20),
        name="add_earlier",
    )(in_hbm(base), other, *got)


def shards(node_states, strengths, start_state, lists, counts):
    groups = lax.axis_size("space")
    slices = lax.axis_size("tm")
    rank = lax.axis_index("space")
    blocks = lists.shape[0] // groups
    list_len = lists.shape[1]
    nodes = in_hbm(node_states.reshape(9, blocks, LANES))
    strengths, start_state = in_hbm(strengths), in_hbm(start_state)

    owner, block = lists // blocks, lists % blocks
    mine = owner == rank
    lowest = jnp.min(jnp.where(mine, block, blocks - 1).reshape(groups, -1), axis=1)
    highest = jnp.max(jnp.where(mine, block, 0).reshape(groups, -1), axis=1)
    send = pl.pallas_call(
        gather_kernel,
        out_shape=jax.ShapeDtypeStruct((groups, 24, LANES), f32),
        in_specs=[smem(), hbm(), hbm()],
        out_specs=vmem(),
        scratch_shapes=[
            pltpu.VMEM((9, blocks, LANES), f32),
            pltpu.VMEM((3, blocks * LANES), f32),
            pltpu.SemaphoreType.DMA((2,)),
        ],
        compiler_params=pltpu.CompilerParams(vmem_limit_bytes=8 << 20),
        name="gather_blocks",
    )(jnp.stack([lowest, highest]), nodes, strengths)
    far = lax.all_to_all(send, "space", 0, 0, tiled=True)

    my_lists = lax.dynamic_slice_in_dim(lists, rank * blocks, blocks, 0)
    owner, block = my_lists.reshape(-1) // blocks, my_lists.reshape(-1) % blocks
    from_shard = owner[None, :] == jnp.arange(groups, dtype=jnp.int32)[:, None]
    first = jnp.min(jnp.where(from_shard, block[None, :], blocks - 1), axis=1)
    first = jnp.sum(jnp.where(from_shard, first[:, None], 0), axis=0)
    slot = jnp.where(
        owner == rank, block, blocks + 2 * owner + (block != first).astype(jnp.int32)
    ).reshape(blocks, list_len)
    near = (slot < blocks).astype(jnp.int32)
    order = jnp.arange(list_len, dtype=jnp.int32)
    ahead = order[None, :] < order[:, None]
    near_ahead = jnp.sum(jnp.where(ahead[None], near[:, None, :], 0), axis=2)
    near_count = jnp.sum(near, axis=1, keepdims=True)
    place = jnp.where(near == 1, near_ahead, near_count + order[None, :] - near_ahead)
    hit = place[:, None, :] == order[None, :, None]
    table = jnp.sum(jnp.where(hit, slot[:, None, :], 0), axis=2).reshape(-1)
    count, number = near_count[:, 0], jnp.arange(blocks, dtype=jnp.int32)
    before = (count[None, :] > count[:, None]) | (
        (count[None, :] == count[:, None]) & (number[None, :] < number[:, None])
    )
    at = jnp.sum(before.astype(jnp.int32), axis=1)
    sorted_targets = jnp.sum(jnp.where(at[None, :] == number[:, None], number[None, :], 0), axis=1)
    last = jnp.arange(2 * TOGETHER - 1, blocks, 2 * TOGETHER, dtype=jnp.int32)
    early = jnp.sum(jnp.where(at[None, :] == last[:, None], count[None, :] // 2, 0), axis=1)
    table = jnp.concatenate([table, jnp.minimum(early, MOST_EARLY), sorted_targets])

    kept = (
        ((blocks, LANES, LANES), bf16),
        ((blocks, 3, 32, LANES), bf16),
        ((blocks, 3, LANES, LANES), bf16),
        ((blocks, 3, 8, LANES), f32),
    )
    near_results = pl.pallas_call(
        near_kernel,
        out_shape=tuple(pltpu.HBM(*k) for k in kept),
        in_specs=[smem(), hbm(), hbm()],
        out_specs=(hbm(),) * 4,
        scratch_shapes=[pltpu.VMEM(*k) for k in kept]
        + [
            pltpu.VMEM((9, blocks, LANES), f32),
            pltpu.VMEM((3, blocks * LANES), f32),
            pltpu.SemaphoreType.DMA((4,)),
        ],
        compiler_params=pltpu.CompilerParams(vmem_limit_bytes=16 << 20),
        cost_estimate=pl.CostEstimate(
            flops=10_000_000_000, bytes_accessed=6_000_000, transcendentals=0
        ),
        name="near_rates",
    )(table, nodes, strengths)

    slots = blocks + 2 * groups
    base, step = pl.pallas_call(
        rest_kernel,
        out_shape=(
            pltpu.HBM((9, blocks, LANES), f32),
            jax.ShapeDtypeStruct((3, blocks, LANES), f32),
        ),
        in_specs=[smem()] * 2 + [vmem()] + [hbm()] * 6,
        out_specs=(hbm(), vmem()),
        scratch_shapes=[
            pltpu.VMEM((slots, LANES, LANES), bf16),
            pltpu.VMEM((slots, 3, 32, LANES), bf16),
            pltpu.VMEM(*kept[2]),
            pltpu.VMEM(*kept[3]),
            pltpu.VMEM((9, blocks, LANES), f32),
            pltpu.VMEM((3, blocks * LANES), f32),
            pltpu.VMEM((9, blocks, LANES), f32),
            pltpu.SemaphoreType.DMA((6,)),
        ],
        compiler_params=pltpu.CompilerParams(vmem_limit_bytes=24 << 20),
        name="rest_rates",
    )(table, counts, far, *map(in_hbm, near_results), nodes, start_state)

    return add_earlier(base, step, slices).reshape(1, 9, blocks * LANES)


def solution(mesh):
    return jax.shard_map(
        shards,
        mesh=mesh,
        in_specs=(P("tm", None, "space"), P(None, "space"), P(None, "space"), P(), P()),
        out_specs=P("tm", None, "space"),
        check_vma=False,
    )
```

```python
import functools
import math

import jax
import jax.numpy as jnp
import numpy as np
from jax import lax
from jax.experimental import pallas as pl
from jax.experimental.pallas import tpu as pltpu
from jax.sharding import PartitionSpec as P

core_sq = 0.25
step_size = 1.0
LANES = 128
ROWS = 16
LIST = 12
TOGETHER = 4
MOST_EARLY = 2
bf16 = jnp.bfloat16
f32 = jnp.float32


def radau_matrix():
    sqrt_six = math.sqrt(6.0)
    return np.array(
        [
            [
                (88.0 - 7.0 * sqrt_six) / 360.0,
                (296.0 - 169.0 * sqrt_six) / 1800.0,
                (-2.0 + 3.0 * sqrt_six) / 225.0,
            ],
            [
                (296.0 + 169.0 * sqrt_six) / 1800.0,
                (88.0 + 7.0 * sqrt_six) / 360.0,
                (-2.0 - 3.0 * sqrt_six) / 225.0,
            ],
            [(16.0 - sqrt_six) / 36.0, (16.0 + sqrt_six) / 36.0, 1.0 / 9.0],
        ]
    )


def pieces(value):
    first = value.astype(bf16)
    rest = value - first.astype(f32)
    second = rest.astype(bf16)
    third = (rest - second.astype(f32)).astype(bf16)
    return first, second, third


def norm_rows(rows, extra):
    square = rows * rows
    norm = square + pltpu.roll(square, ROWS - 1, 0) + pltpu.roll(square, ROWS - 2, 0) + extra
    first, second, third = [piece.astype(f32) for piece in pieces(norm)]
    place = lax.broadcasted_iota(jnp.int32, (ROWS, LANES), 0) % 3
    return jnp.where(
        place == 0,
        first,
        jnp.where(place == 1, pltpu.roll(second, 1, 0), pltpu.roll(third, 2, 0)),
    )


def cross(former, latter):
    return [
        former[1] * latter[2] - former[2] * latter[1],
        former[2] * latter[0] - former[0] * latter[2],
        former[0] * latter[1] - former[1] * latter[0],
    ]


def source_features(rows, feature_ref, weight_ref, slot):
    first, second, third = [(-2.0 * piece.astype(f32)).astype(bf16) for piece in pieces(rows)]
    norms = norm_rows(rows, core_sq).astype(bf16)
    ones = jnp.ones((ROWS, LANES), bf16)
    stacked = jnp.concatenate([first, second, first, second, third, first, norms, ones], 0)
    feature_ref[slot] = stacked.T
    place = lax.broadcasted_iota(jnp.int32, (ROWS, LANES), 0)

    def turned(value):
        ahead = jnp.where(place % 3 == 2, pltpu.roll(value, 2, 0), pltpu.roll(value, ROWS - 1, 0))
        behind = jnp.where(place % 3 == 0, pltpu.roll(value, ROWS - 2, 0), pltpu.roll(value, 1, 0))
        return ahead, behind

    strength = jnp.where(
        place < 3,
        pltpu.roll(rows, ROWS - 9, 0),
        jnp.where(place < 6, pltpu.roll(rows, ROWS - 6, 0), pltpu.roll(rows, ROWS - 3, 0)),
    )
    ahead, behind = turned(rows)
    strength_ahead, strength_behind = turned(strength)
    weights = jnp.where(place < 9, ahead * strength_behind - behind * strength_ahead, rows)
    parts = [piece.astype(f32) for piece in pieces(weights)]
    top = place < 3
    blank = jnp.zeros((8, LANES), f32)
    for m in range(3):
        made = [
            jnp.where(top, pltpu.roll(p, (ROWS - 3 * m) % ROWS, 0), pltpu.roll(p, ROWS - 6, 0))[0:8]
            for p in parts
        ]
        weight_ref[slot, m] = jnp.concatenate(made + [blank, blank, made[2]], 0).astype(bf16)


def target_features(rows, target_ref, t):
    first, second, third = [piece.astype(f32) for piece in pieces(rows)]
    norms = norm_rows(rows, 0.0)
    place = lax.broadcasted_iota(jnp.int32, (ROWS, LANES), 0)
    ones = jnp.ones((ROWS, LANES), f32)
    groups = (first, first, second, second, first, third, ones, norms)
    for m in range(3):
        node = (place >= 3 * m) & (place < 3 * m + 3)
        target_ref[t, m] = jnp.concatenate(
            [jnp.where(node, g, 0.0).astype(bf16) for g in groups], 0
        )


def lanes_of(t):
    return pl.ds(pl.multiple_of(t * LANES, LANES), LANES)


def pair_sums(table_ref, target_ref, feature_ref, weight_ref, ids, m, begin, end):
    list_len = LIST
    zero = jnp.zeros((LANES, LANES), bf16)
    both = jnp.concatenate(
        [
            jnp.concatenate([target_ref[ids[0], m], zero], 1),
            jnp.concatenate([zero, target_ref[ids[1], m]], 1),
        ],
        0,
    )
    total = jnp.zeros((48, 2 * LANES), f32)
    for j in range(begin, end, 2):
        slots = [[table_ref[t * list_len + q] for q in (j, j + 1)] for t in ids]
        features = jnp.concatenate(
            [
                jnp.concatenate([feature_ref[slots[0][q]], feature_ref[slots[1][q]]], 1)
                for q in range(2)
            ],
            0,
        )
        ones, twos = [
            jnp.concatenate([weight_ref[s[0], m], weight_ref[s[1], m]], 1) for s in slots
        ]
        weights = jnp.concatenate([ones[0:16], twos[0:16], ones[16:32] + twos[32:48]], 0)
        squares = jnp.dot(features, both, preferred_element_type=f32)
        inverse = lax.rsqrt(squares)
        kernel = inverse * inverse * inverse
        high = kernel.astype(bf16)
        low = (kernel - high.astype(f32)).astype(bf16)
        total = total + jnp.dot(weights, high, preferred_element_type=f32)
        total = total + jnp.dot(weights, low, preferred_element_type=f32)
    sums = []
    for q in range(2):
        mine = total[:, LANES * q : LANES * q + LANES]
        sums.append(mine[16 * q : 16 * q + 8] + mine[16 * q + 8 : 16 * q + 16] + mine[32 + 8 * q : 40 + 8 * q])
    return sums


def fetch(pairs, sems):
    copies = [pltpu.make_async_copy(a, b, sems.at[k]) for k, (a, b) in enumerate(pairs)]
    for copy in copies:
        copy.start()
    return copies


def group_pairs(table_ref, early, blocks, i):
    first = early + blocks // (2 * TOGETHER) + 2 * TOGETHER * i
    ids = [table_ref[first + k] for k in range(2 * TOGETHER)]
    return [(ids[2 * k], ids[2 * k + 1]) for k in range(TOGETHER)]


def gather_kernel(pick_ref, node_in, strength_in, send_ref, node_ref, strength_ref, sems):
    for copy in fetch(((node_in, node_ref), (strength_in, strength_ref)), sems):
        copy.wait()

    def one(d, _):
        for k in range(2):
            lanes = lanes_of(pick_ref[k, d])
            send_ref[d, 12 * k : 12 * k + 9] = node_ref[:, pick_ref[k, d], :]
            send_ref[d, 12 * k + 9 : 12 * k + 12] = strength_ref[:, lanes]
        return 0

    lax.fori_loop(0, send_ref.shape[0], one, 0, unroll=4)


def near_kernel(
    table_ref,
    node_in,
    strength_in,
    feature_out,
    weight_out,
    target_out,
    part_out,
    feature_ref,
    weight_ref,
    target_ref,
    part_ref,
    node_ref,
    strength_ref,
    sems,
):
    blocks = part_ref.shape[0]
    early = LIST * blocks
    for copy in fetch(((node_in, node_ref), (strength_in, strength_ref)), sems):
        copy.wait()

    def prepare(t, _):
        lanes = lanes_of(t)
        rows = jnp.concatenate(
            [node_ref[:, t, :], strength_ref[:, lanes], jnp.zeros((4, LANES), f32)], 0
        )
        source_features(rows, feature_ref, weight_ref, t)
        target_features(rows, target_ref, t)
        return 0

    lax.fori_loop(0, blocks, prepare, 0, unroll=4)
    kept = ((feature_ref, feature_out), (weight_ref, weight_out), (target_ref, target_out))
    copies = fetch(kept, sems)

    def group(i, _):
        for steps in range(MOST_EARLY + 1):

            @pl.when(table_ref[early + i] == steps)
            def _():
                made = []
                for ids in group_pairs(table_ref, early, blocks, i):
                    for m in range(3):
                        sums = pair_sums(
                            table_ref, target_ref, feature_ref, weight_ref, ids, m, 0, 2 * steps
                        )
                        made.extend((t, m, value) for t, value in zip(ids, sums))
                for t, m, value in made:
                    part_ref[t, m] = value

        return 0

    lax.fori_loop(0, blocks // (2 * TOGETHER), group, 0)
    copies.append(pltpu.make_async_copy(part_ref, part_out, sems.at[3]))
    copies[3].start()
    for copy in copies:
        copy.wait()


def rest_kernel(
    table_ref,
    count_ref,
    far_ref,
    near_feature,
    near_weight,
    near_target,
    near_part,
    node_in,
    start_in,
    base_out,
    step_ref,
    feature_ref,
    weight_ref,
    target_ref,
    part_ref,
    node_ref,
    start_ref,
    base_ref,
    sems,
):
    blocks = part_ref.shape[0]
    early = LIST * blocks
    radau = radau_matrix() * step_size

    def far_source(i, _):
        blank = jnp.zeros((4, LANES), f32)
        for k in range(2):
            rows = jnp.concatenate([far_ref[i, 12 * k : 12 * k + 12], blank], 0)
            source_features(rows, feature_ref, weight_ref, blocks + 2 * i + k)
        return 0

    kept = (
        (near_feature, feature_ref.at[0:blocks]),
        (near_weight, weight_ref.at[0:blocks]),
        (near_target, target_ref),
        (near_part, part_ref),
        (node_in, node_ref),
        (start_in, start_ref),
    )
    copies = fetch(kept, sems)
    lax.fori_loop(0, far_ref.shape[0], far_source, 0, unroll=2)
    for copy in copies:
        copy.wait()
    live = count_ref[lax.axis_index("space")]

    def group(i, _):
        for steps in range(MOST_EARLY + 1):

            @pl.when(table_ref[early + i] == steps)
            def _():
                made = []
                for ids in group_pairs(table_ref, early, blocks, i):
                    for m in range(3):
                        sums = pair_sums(
                            table_ref, target_ref, feature_ref, weight_ref, ids, m, 2 * steps, LIST
                        )
                        made.extend((t, m, value) for t, value in zip(ids, sums))
                for t, m, value in made:
                    part_ref[t, m] = part_ref[t, m] + value

        return 0

    def close(t, _):
        rows = node_ref[:, t, :]
        start = start_ref[:, lanes_of(t)]
        on = jnp.where(t < live, 1.0, 0.0).astype(f32)
        velocity = []
        for m in range(3):
            sums = part_ref[t, m]
            place = [rows[3 * m + c : 3 * m + c + 1] for c in range(3)]
            spread = cross(place, [sums[3 + c : 4 + c] for c in range(3)])
            velocity.append([(spread[c] - sums[c : c + 1]) * (-0.25 / math.pi) for c in range(3)])
        for k in range(3):
            for c in range(3):
                step = sum(float(radau[k, n]) * velocity[n][c] for n in range(3)) * on
                base_ref[3 * k + c, pl.ds(t, 1), :] = start[c : c + 1] + step
                if k == 2:
                    step_ref[c, pl.ds(t, 1), :] = step
        return 0

    lax.fori_loop(0, blocks // (2 * TOGETHER), group, 0)
    lax.fori_loop(0, blocks, close, 0, unroll=4)
    (copy,) = fetch(((base_ref, base_out),), sems)
    copy.wait()


def hbm():
    return pl.BlockSpec(memory_space=pltpu.HBM)


def in_hbm(value):
    return pltpu.with_memory_space_constraint(value, pltpu.HBM)


def vmem():
    return pl.BlockSpec(memory_space=pltpu.VMEM)


def smem():
    return pl.BlockSpec(memory_space=pltpu.SMEM)


def sum_kernel(shifts, base_in, other_ref, *refs):
    got_refs, (out_ref, base_ref, sems) = refs[:-3], refs[-3:]
    (copy,) = fetch(((base_in, base_ref),), sems)
    rank = lax.axis_index("tm")

    def keep(value, k):
        return jnp.where((rank ^ k) < rank, 1.0, 0.0).astype(f32) * value

    carried = keep(other_ref[...], 1)
    for k, ref in zip(shifts, got_refs):
        carried = carried + keep(ref[...], k)
    copy.wait()
    for m in range(3):
        out_ref[3 * m : 3 * m + 3] = base_ref[3 * m : 3 * m + 3] + carried


def add_earlier(base, step, slices):
    def swap(value, k):
        return lax.ppermute(value, "tm", [(i, i ^ k) for i in range(slices)])

    other = swap(step, 1)
    chip = step + other
    shifts = tuple(range(2, slices, 2))
    got = [swap(chip, k) for k in shifts]
    return pl.pallas_call(
        functools.partial(sum_kernel, shifts),
        out_shape=jax.ShapeDtypeStruct(base.shape, f32),
        in_specs=[hbm()] + [vmem()] * (1 + len(got)),
        out_specs=vmem(),
        scratch_shapes=[pltpu.VMEM(base.shape, f32), pltpu.SemaphoreType.DMA((1,))],
        compiler_params=pltpu.CompilerParams(vmem_limit_bytes=8 << 20),
        name="add_earlier",
    )(in_hbm(base), other, *got)


def shards(node_states, strengths, start_state, lists, counts):
    groups = lax.axis_size("space")
    slices = lax.axis_size("tm")
    rank = lax.axis_index("space")
    blocks = lists.shape[0] // groups
    list_len = lists.shape[1]
    nodes = in_hbm(node_states.reshape(9, blocks, LANES))
    strengths, start_state = in_hbm(strengths), in_hbm(start_state)

    owner, block = lists // blocks, lists % blocks
    mine = owner == rank
    lowest = jnp.min(jnp.where(mine, block, blocks - 1).reshape(groups, -1), axis=1)
    highest = jnp.max(jnp.where(mine, block, 0).reshape(groups, -1), axis=1)
    send = pl.pallas_call(
        gather_kernel,
        out_shape=jax.ShapeDtypeStruct((groups, 24, LANES), f32),
        in_specs=[smem(), hbm(), hbm()],
        out_specs=vmem(),
        scratch_shapes=[
            pltpu.VMEM((9, blocks, LANES), f32),
            pltpu.VMEM((3, blocks * LANES), f32),
            pltpu.SemaphoreType.DMA((2,)),
        ],
        compiler_params=pltpu.CompilerParams(vmem_limit_bytes=8 << 20),
        name="gather_blocks",
    )(jnp.stack([lowest, highest]), nodes, strengths)
    far = lax.all_to_all(send, "space", 0, 0, tiled=True)

    my_lists = lax.dynamic_slice_in_dim(lists, rank * blocks, blocks, 0)
    owner, block = my_lists.reshape(-1) // blocks, my_lists.reshape(-1) % blocks
    from_shard = owner[None, :] == jnp.arange(groups, dtype=jnp.int32)[:, None]
    first = jnp.min(jnp.where(from_shard, block[None, :], blocks - 1), axis=1)
    first = jnp.sum(jnp.where(from_shard, first[:, None], 0), axis=0)
    slot = jnp.where(
        owner == rank, block, blocks + 2 * owner + (block != first).astype(jnp.int32)
    ).reshape(blocks, list_len)
    near = (slot < blocks).astype(jnp.int32)
    order = jnp.arange(list_len, dtype=jnp.int32)
    ahead = order[None, :] < order[:, None]
    near_ahead = jnp.sum(jnp.where(ahead[None], near[:, None, :], 0), axis=2)
    near_count = jnp.sum(near, axis=1, keepdims=True)
    place = jnp.where(near == 1, near_ahead, near_count + order[None, :] - near_ahead)
    hit = place[:, None, :] == order[None, :, None]
    table = jnp.sum(jnp.where(hit, slot[:, None, :], 0), axis=2).reshape(-1)
    count, number = near_count[:, 0], jnp.arange(blocks, dtype=jnp.int32)
    before = (count[None, :] > count[:, None]) | (
        (count[None, :] == count[:, None]) & (number[None, :] < number[:, None])
    )
    at = jnp.sum(before.astype(jnp.int32), axis=1)
    sorted_targets = jnp.sum(jnp.where(at[None, :] == number[:, None], number[None, :], 0), axis=1)
    last = jnp.arange(2 * TOGETHER - 1, blocks, 2 * TOGETHER, dtype=jnp.int32)
    early = jnp.sum(jnp.where(at[None, :] == last[:, None], count[None, :] // 2, 0), axis=1)
    table = jnp.concatenate([table, jnp.minimum(early, MOST_EARLY), sorted_targets])

    kept = (
        ((blocks, LANES, LANES), bf16),
        ((blocks, 3, 48, LANES), bf16),
        ((blocks, 3, LANES, LANES), bf16),
        ((blocks, 3, 8, LANES), f32),
    )
    near_results = pl.pallas_call(
        near_kernel,
        out_shape=tuple(pltpu.HBM(*k) for k in kept),
        in_specs=[smem(), hbm(), hbm()],
        out_specs=(hbm(),) * 4,
        scratch_shapes=[pltpu.VMEM(*k) for k in kept]
        + [
            pltpu.VMEM((9, blocks, LANES), f32),
            pltpu.VMEM((3, blocks * LANES), f32),
            pltpu.SemaphoreType.DMA((4,)),
        ],
        compiler_params=pltpu.CompilerParams(vmem_limit_bytes=16 << 20),
        cost_estimate=pl.CostEstimate(
            flops=10_000_000_000, bytes_accessed=6_000_000, transcendentals=0
        ),
        name="near_rates",
    )(table, nodes, strengths)

    slots = blocks + 2 * groups
    base, step = pl.pallas_call(
        rest_kernel,
        out_shape=(
            pltpu.HBM((9, blocks, LANES), f32),
            jax.ShapeDtypeStruct((3, blocks, LANES), f32),
        ),
        in_specs=[smem()] * 2 + [vmem()] + [hbm()] * 6,
        out_specs=(hbm(), vmem()),
        scratch_shapes=[
            pltpu.VMEM((slots, LANES, LANES), bf16),
            pltpu.VMEM((slots, 3, 48, LANES), bf16),
            pltpu.VMEM(*kept[2]),
            pltpu.VMEM(*kept[3]),
            pltpu.VMEM((9, blocks, LANES), f32),
            pltpu.VMEM((3, blocks * LANES), f32),
            pltpu.VMEM((9, blocks, LANES), f32),
            pltpu.SemaphoreType.DMA((6,)),
        ],
        compiler_params=pltpu.CompilerParams(vmem_limit_bytes=24 << 20),
        name="rest_rates",
    )(table, counts, far, *map(in_hbm, near_results), nodes, start_state)

    return add_earlier(base, step, slices).reshape(1, 9, blocks * LANES)


def solution(mesh):
    return jax.shard_map(
        shards,
        mesh=mesh,
        in_specs=(P("tm", None, "space"), P(None, "space"), P(None, "space"), P(), P()),
        out_specs=P("tm", None, "space"),
        check_vma=False,
    )
```
